32 devices in a mesh: gx: 8 (over y, x, core), sp: 4 (over z).
Axes of the slice: x: 2, y: 2, z: 4, core: 2. Of those that a mesh axis runs over, the one named last changes fastest.
Arguments:
- previous_head: float32 [8, 64, 512], P(None, 'gx', 'sp'), may hold values from -6 to 6
- recharge: float32 [8, 64, 512], P(None, 'gx', 'sp'), may hold values from -6 to 6
- soil_zone: int32 [8, 64, 512], P(None, 'gx', 'sp'), may hold values from 0 to 7
- soil_cond: float32 [8], replicated, may hold values from 0.1 to 1
- soil_store: float32 [8], replicated, may hold values from 0.05 to 0.5
- species: float32 [12, 8, 64, 512], P('sp', None, 'gx'), may hold values from -6 to 6
- mineral_zone: int32 [8, 64, 512], P(None, 'gx', 'sp'), may hold values from 0 to 5
- rate_table: float32 [6, 8], replicated, may hold values from 0.3 to 3
- stoich: float32 [12, 8], replicated, may hold values from -3 to 3
- log_equil: float32 [8], replicated, may hold values from -1 to 1
Outputs:
- head_field: float32 [8, 64, 512], P(None, 'gx', 'sp')
- species_out: float32 [12, 8, 64, 512], P('sp', None, 'gx')
The draws below stay inside these ranges and needn't reach their ends.
Inputs may be any that keep to these rules, and one draw needn't show every extreme that they name: `soil_zone`: a soil class of 8. `mineral_zone`: a mineral zone class of 6.
All inputs are finite; a program needn't handle non-finite values.
Results may differ from the reference program's by a relative error of at most 0.0003.
Values sent between devices are 32-bit elements; how exact they have to be, the bound alone decides.
No kernel may reach another device: no remote copies, remote signals or barrier semaphores. Data moves between devices by JAX's collectives and lax.ppermute only.
A program may use at most 64 MiB of HBM per device.

```python
import math
import jax
import jax.numpy as jnp
from jax import lax

S = 12
NM = 8
NSOIL = 8
NMZONE = 6
NZ = 8
ITERS = 6
NEWTON = 2
NX = 64
NY = 512


def place_ends(values, stream_key, least, high):
    dims = values.shape
    index_at = [jax.random.randint(jax.random.fold_in(stream_key, axis), (), 0, dims[axis]) for axis in range(len(dims))]
    values = values.at[tuple(index_at)].set(least)
    longest = dims.index(max(dims))
    index_at[longest] = (index_at[longest] + 1) % dims[longest]
    return values.at[tuple(index_at)].set(high)


def block_scale(stream_key, extent, pieces, low, top_value):
    gain, own = 1.0, jax.random.fold_in(stream_key, 6)
    for axis_at, blocks in pieces:
        steps = jnp.exp(jax.random.uniform(jax.random.fold_in(own, axis_at), (blocks,), jnp.float32, low / len(pieces), top_value / len(pieces)))
        gain = gain * jnp.repeat(steps, extent[axis_at] // blocks).reshape([-1 if axis == axis_at else 1 for axis in range(len(extent))])
    return gain


def bell_draw(stream_key, shape, deviation, most, shards=(), kind=jnp.bfloat16):
    drawn = jax.random.normal(stream_key, shape, jnp.float32) * deviation
    if len(shards) > 0:
        drawn = block_scale(stream_key, shape, shards, -0.22, 0.18) * drawn
    return jnp.clip(drawn, min=-most, max=most).astype(kind)


def setup_inputs(seed: int = 0) -> dict:
    key_list = jax.random.split(jax.random.key(seed), 11)
    return {
        "previous_head": bell_draw(key_list[0], (NZ, NX, NY), 1.0, 6.0, ((1, 8), (2, 4)), jnp.float32),
        "recharge": bell_draw(key_list[1], (NZ, NX, NY), 1.0, 6.0, ((1, 8), (2, 4)), jnp.float32),
        "soil_zone": place_ends(jax.random.randint(key_list[2], (NZ, NX, NY), 0, NSOIL), jax.random.fold_in(key_list[2], 1), 0, NSOIL - 1).astype(jnp.int32),
        "soil_cond": jnp.clip(jnp.exp(jax.random.uniform(key_list[3], (NSOIL,), jnp.float32, math.log(0.1), math.log(1.0))), 0.1, 1.0),
        "soil_store": jnp.clip(jnp.exp(jax.random.uniform(key_list[4], (NSOIL,), jnp.float32, math.log(0.05), math.log(0.5))), 0.05, 0.5),
        "species": bell_draw(key_list[5], (S, NZ, NX, NY), 1.0, 6.0, ((0, 4), (2, 8)), jnp.float32),
        "mineral_zone": place_ends(jax.random.randint(key_list[6], (NZ, NX, NY), 0, NMZONE), jax.random.fold_in(key_list[6], 1), 0, NMZONE - 1).astype(jnp.int32),
        "rate_table": jnp.clip(jnp.exp(jax.random.uniform(key_list[7], (NMZONE, NM), jnp.float32, math.log(0.3), math.log(3.0))), 0.3, 3.0),
        "stoich": bell_draw(key_list[8], (S, NM), 0.5, 3.0, (), jnp.float32),
        "log_equil": jnp.clip(jax.random.uniform(key_list[9], (NM,), jnp.float32, -1.0, 1.0), -1.0, 1.0),
    }


time_step = 0.05
dispersion = 0.5
reaction_span = 0.5
newton_damping = 0.5

def harmonic(center, other):
    return 2.0 * center * other / (center + other)

def six_sides(padded):
    return [padded[..., 2:, 1:-1, 1:-1], padded[..., :-2, 1:-1, 1:-1], padded[..., 1:-1, 2:, 1:-1], padded[..., 1:-1, :-2, 1:-1], padded[..., 1:-1, 1:-1, 2:], padded[..., 1:-1, 1:-1, :-2]]

def lookup(labels, entries):
    levels = jnp.arange(entries.shape[0], dtype=jnp.int32).reshape((-1,) + (1,) * labels.ndim)
    return lax.optimization_barrier(jnp.sum(jnp.where(labels[None] == levels, entries.reshape(levels.shape), 0.0), axis=0))

def lookup_rows(labels, entries):
    levels = jnp.arange(entries.shape[0], dtype=jnp.int32)[:, None, None]
    return lax.optimization_barrier(jnp.sum(jnp.where(labels[None, None, :] == levels, entries[:, :, None], 0.0), axis=0))

def transport(concentration, conc_padded, head_padded, cond_padded):
    head_center = head_padded[1:-1, 1:-1, 1:-1]
    conduct = cond_padded[1:-1, 1:-1, 1:-1]
    change = jnp.zeros_like(concentration)
    for beside, head_beside, cond_beside in zip(six_sides(conc_padded), six_sides(head_padded), six_sides(cond_padded)):
        face_cond = harmonic(conduct, cond_beside)
        velocity = face_cond * (head_center - head_beside)
        change = change + jnp.maximum(velocity, 0.0) * concentration + jnp.minimum(velocity, 0.0) * beside
        change = change + dispersion * face_cond * (concentration - beside)
    return concentration - time_step * change

def solve_system(jacobian, mismatch):
    dimension = mismatch.shape[0]
    factor = [[None] * dimension for i in range(dimension)]
    inverse = [None] * dimension
    for j in range(dimension):
        for i in range(j, dimension):
            running = jacobian[i * dimension + j] + (1.0 if i == j else 0.0)
            for k in range(j):
                running = running - factor[i][k] * factor[j][k]
            if i == j:
                diag_root = jnp.sqrt(running)
                factor[j][j] = diag_root
                inverse[j] = 1.0 / diag_root
            else:
                factor[i][j] = running * inverse[j]
    forward = []
    for i in range(dimension):
        running = mismatch[i]
        for k in range(i):
            running = running - factor[i][k] * forward[k]
        forward.append(running * inverse[i])
    answer = [None] * dimension
    for i in reversed(range(dimension)):
        running = forward[i]
        for k in range(i + 1, dimension):
            running = running - factor[k][i] * answer[k]
        answer[i] = running * inverse[i]
    return jnp.stack(answer, 0)

def reaction(concentration, labels, rate_table, stoich, log_equil):
    rate_cells = lookup_rows(labels, rate_table)
    pair_products = (stoich[:, None, :] * stoich[None, :, :]).reshape(-1, stoich.shape[1])
    iterate = concentration
    for newton_pass in range(NEWTON):
        affinity = jnp.dot(stoich.T, iterate, precision=lax.Precision.HIGHEST, preferred_element_type=jnp.float32) - log_equil[:, None]
        tangent = jnp.tanh(affinity)
        mismatch = iterate - concentration + reaction_span * jnp.dot(stoich, rate_cells * tangent, precision=lax.Precision.HIGHEST, preferred_element_type=jnp.float32)
        jacobian = reaction_span * jnp.dot(pair_products, rate_cells * (1.0 - tangent * tangent), precision=lax.Precision.HIGHEST, preferred_element_type=jnp.float32)
        iterate = iterate - newton_damping * solve_system(jacobian, mismatch)
    return iterate

def flow_operator(field, storage, faces):
    padded = jnp.pad(field, 1)
    result = storage * field
    for face_cond, beside in zip(faces, six_sides(padded)):
        result = result + face_cond * (field - beside)
    return result

def reference(previous_head, recharge, soil_zone, soil_cond, soil_store, species, mineral_zone, rate_table, stoich, log_equil):
    conduct = lookup(soil_zone, soil_cond)
    storage = lookup(soil_zone, soil_store)
    cond_padded = jnp.pad(conduct, 1)
    faces = [harmonic(conduct, beside) for beside in six_sides(cond_padded)]
    source = storage * previous_head + recharge
    head_field = jnp.zeros_like(source)
    residual = source
    direction = source
    norm_now = jnp.sum(residual * residual)
    for iteration in range(ITERS):
        image = flow_operator(direction, storage, faces)
        alpha = norm_now / jnp.sum(direction * image)
        head_field = head_field + alpha * direction
        residual = residual - alpha * image
        norm_next = jnp.sum(residual * residual)
        direction = residual + norm_next / norm_now * direction
        norm_now = norm_next
    head_padded = jnp.pad(head_field, 1)
    moved = lax.map(lambda single: transport(single, jnp.pad(single, 1), head_padded, cond_padded), species)
    layers = moved.transpose(1, 0, 2, 3).reshape(NZ, S, NX * NY)
    labels = mineral_zone.reshape(NZ, NX * NY)
    reacted = lax.map(lambda couple: reaction(couple[0], couple[1], rate_table, stoich, log_equil), (layers, labels))
    species_out = reacted.reshape(NZ, S, NX, NY).transpose(1, 0, 2, 3)
    return (head_field, species_out)
```

```python
import functools

import jax
import jax.numpy as jnp
from jax import lax
from jax.experimental import pallas as pl
from jax.experimental.pallas import tpu as pltpu
from jax.sharding import PartitionSpec as P

ITERS = 6
NEWTON = 2

time_step = 0.05
dispersion = 0.5
reaction_span = 0.5
newton_damping = 0.5

LANES = 128
BASIS = ITERS + 1
PAIRS = [(i, j) for j in range(BASIS) for i in range(j + 1)]
PAIR_AT = {pair: at for at, pair in enumerate(PAIRS)}
PAIR_ROWS = -(-len(PAIRS) // 8) * 8


def harmonic(center, other):
    return 2.0 * center * other / jnp.maximum(center + other, 1e-30)


def pick(labels, table, first):
    value = jnp.zeros(labels.shape, jnp.float32)
    for level in range(table.shape[0]):
        value = jnp.where(labels == level + first, table[level], value)
    return value


def lane_ids(shape):
    return lax.broadcasted_iota(jnp.int32, shape, len(shape) - 1)


def pack_kernel(cond_t, store_t, previous, recharge, zone, species, *outs):
    *blocks, stats = outs
    count = len(blocks)
    me = lax.axis_index("sp")
    groups, layers = species.shape[0], species.shape[1]
    shape = previous.shape[1:]
    lane = lane_ids(shape)
    conduct, store_sum, face_sum = [], jnp.zeros(shape), jnp.zeros(shape)
    for z in range(layers):
        labels = zone[z]
        conduct.append(pick(labels, cond_t, 0))
        storage = pick(labels, store_t, 0)
        store_sum = store_sum + storage
        source = storage * previous[z] + recharge[z]
        label = (labels + 1).astype(jnp.float32)
        for d in {1, count - 1}:
            blocks[d][z] = source
            blocks[d][layers + z] = label
    for z in range(layers):
        face_sum = face_sum + 8.0 * harmonic(conduct[z], pltpu.roll(conduct[z], 1, 0))
        if z + 1 < layers:
            face_sum = face_sum + 4.0 * harmonic(conduct[z], conduct[z + 1])
    column = jnp.sum(store_sum + face_sum, axis=0, keepdims=True) * (1.0 / (layers * shape[0]))
    stats[...] = jnp.broadcast_to(jnp.max(column, axis=1, keepdims=True), stats.shape)

    for d in range(count):
        base = blocks[d].shape[0] - groups * layers - 1
        here = lax.rem(me + d, count)
        left = lax.rem(here + count - 1, count)
        right = lax.rem(here + 1, count)
        at = [pl.ds(pl.multiple_of(i * LANES, LANES), LANES) for i in (left, here, right)]
        edge = jnp.zeros(shape, jnp.float32)
        for c in range(groups):
            for z in range(layers):
                j = c * layers + z
                blocks[d][base + j] = species[c, z, :, at[1]]
                edge = jnp.where(lane == 2 * j, pltpu.roll(species[c, z, :, at[2]], 2 * j, 1), edge)
                edge = jnp.where(
                    lane == 2 * j + 1, pltpu.roll(species[c, z, :, at[0]], 2 * j + 2, 1), edge
                )
        blocks[d][base + groups * layers] = edge


def widen_kernel(groups, own_field, *refs):
    *blocks, up, down = refs
    count = len(blocks)
    me = lax.axis_index("sp")
    layers = (blocks[1].shape[0] - blocks[0].shape[0]) // 2
    rows = own_field.shape[1]
    has_left = (me > 0).astype(jnp.float32)
    has_right = (me < count - 1).astype(jnp.float32)
    lane = lane_ids(own_field.shape[1:])
    for t in range(2 * layers):
        near = jnp.where(lane < LANES // 2, blocks[count - 1][t] * has_right, blocks[1][t] * has_left)
        for out in (up, down):
            out[t] = own_field[t]
            out[2 * layers + t] = near
    for d in range(count):
        base = blocks[d].shape[0] - groups * layers - 1
        for c in range(groups):
            at = 4 * layers + d * groups + c
            span = pl.ds(base + c * layers, layers)
            up[at] = blocks[d][span, 0, :]
            down[at] = blocks[d][span, rows - 1, :]


def krylov_kernel(cond_t, store_t, stats, own, above, below, basis, kx, ky, kz, sums, cond_s, store_s, pair_s):
    count = lax.axis_size("gx")
    me = lax.axis_index("gx")
    layers, tall, wide = cond_s.shape
    rows = tall // 3
    keep = ((me > 0).astype(jnp.float32), 1.0, (me < count - 1).astype(jnp.float32))
    top = jnp.max(stats[...], axis=0, keepdims=True)
    top = jnp.concatenate([top] * (wide // LANES), axis=1)
    twice, fourth = 2.0 / top, 4.0 / top

    for z in range(layers):
        for part, (block, use) in enumerate(zip((above, own, below), keep)):
            at = slice(part * rows, (part + 1) * rows)
            for half in range(2):
                cols = slice(half * LANES, (half + 1) * LANES)
                field = block[2 * layers * half + z]
                labels = block[2 * layers * half + layers + z]
                if part != 1:
                    field, labels = field * use, labels * use
                basis[0, z, at, cols] = field
                cond_s[z, at, cols] = pick(labels, cond_t, 1)
                store_s[z, at, cols] = pick(labels, store_t, 1)
    kz[0] = jnp.zeros((tall, wide), jnp.float32)
    for z in range(layers):
        here = cond_s[z]
        kx[z] = harmonic(here, pltpu.roll(here, tall - 1, 0))
        ky[z] = harmonic(here, pltpu.roll(here, wide - 1, 1))
        if z + 1 < layers:
            kz[z + 1] = harmonic(here, cond_s[z + 1])

    def operate(k):
        flow = None
        result = []
        for z in range(layers):
            value = basis[k, z]
            along_x = kx[z] * (value - pltpu.roll(value, tall - 1, 0))
            along_y = ky[z] * (value - pltpu.roll(value, wide - 1, 1))
            image = store_s[z] * value
            image = image + (along_x - pltpu.roll(along_x, 1, 0))
            image = image + (along_y - pltpu.roll(along_y, 1, 1))
            if z + 1 < layers:
                along_z = kz[z + 1] * (value - basis[k, z + 1])
                image = image + along_z
            if z:
                image = image - flow
            flow = along_z
            yield z, value, image

    for z, value, image in operate(0):
        basis[1, z] = image * twice - value

    def step(k, carry):
        for z, value, image in operate(k):
            basis[k + 1, z] = image * fourth - 2.0 * value - basis[k - 1, z]
        return carry

    lax.fori_loop(1, ITERS, step, 0)

    totals = [None] * len(PAIRS)
    for z in range(layers):
        values = [basis[k, z, rows : 2 * rows, :LANES] for k in range(BASIS)]
        for at, (i, j) in enumerate(PAIRS):
            term = values[i] * values[j]
            totals[at] = term if z == 0 else totals[at] + term
    pair_s[...] = jnp.zeros(pair_s.shape, jnp.float32)
    for at, total in enumerate(totals):
        pair_s[at : at + 1, :] = jnp.sum(total, axis=0, keepdims=True)
    full = jnp.sum(pair_s[...], axis=1, keepdims=True)
    lane = lane_ids(pair_s.shape)
    row = lax.broadcasted_iota(jnp.int32, pair_s.shape, 0)
    line = jnp.sum(jnp.where(lane == row, full, 0.0), axis=0, keepdims=True)
    sums[...] = jnp.broadcast_to(line, sums.shape)


def direction_weights(gram, cap):
    def inner(i, j):
        return gram[PAIR_AT[(min(i, j), max(i, j))]]

    def image_inner(i, j):
        if j == 0:
            return 2.0 * (inner(i, 0) + inner(i, 1))
        return inner(i, j + 1) + inner(i, j - 1) + 2.0 * inner(i, j)

    def quadratic(values, form):
        total = None
        for i, left in enumerate(values):
            part = form(i, i) * left
            for j in range(i):
                part = part + 2.0 * form(i, j) * values[j]
            total = left * part if total is None else total + left * part
        return total

    images = {(i, j): image_inner(i, j) for i in range(ITERS) for j in range(i + 1)}
    start = inner(0, 0)
    one = jnp.ones_like(start)
    zero = jnp.zeros_like(start)
    head, residual, direction = [zero] * ITERS, [one], [one]
    norm_now = start
    live = norm_now > 0.0
    for iteration in range(ITERS):
        product = quadratic(direction, lambda i, j: images[(i, j)])
        live = jnp.logical_and(live, product > 0.0)
        alpha = jnp.where(live, jnp.minimum(norm_now / jnp.where(live, product, one), cap), zero)
        for i, part in enumerate(direction):
            head[i] = head[i] + alpha * part
        if iteration + 1 == ITERS:
            return head
        applied = [zero] * (iteration + 2)
        for j, part in enumerate(direction):
            applied[j] = applied[j] + 2.0 * part
            applied[j + 1] = applied[j + 1] + (2.0 * part if j == 0 else part)
            if j:
                applied[j - 1] = applied[j - 1] + part
        residual = residual + [zero]
        residual = [part - alpha * moved for part, moved in zip(residual, applied)]
        norm_next = jnp.maximum(quadratic(residual, inner), 0.0)
        ratio = norm_next / jnp.where(live, norm_now, one)
        live = jnp.logical_and(live, norm_next > 1e-7 * start)
        direction = [part + ratio * past for part, past in zip(residual, direction + [zero])]
        norm_now = norm_next


def react(moved, rates, powers, stoich, rows, log_equil):
    minerals = len(rates)
    first = []
    for m in range(minerals):
        total = None
        for value, row in zip(moved, rows):
            term = stoich[row, m] * value
            total = term if total is None else total + term
        first.append(total - log_equil[m])
    shift = None
    for newton_pass in range(NEWTON):
        if shift is None:
            affinity = first
        else:
            affinity = []
            for m in range(minerals):
                total = first[m]
                for n in range(minerals):
                    total = total - powers[m, n] * shift[n]
                affinity.append(total)
        tangent = [jnp.tanh(value) for value in affinity]
        gap = [reaction_span * rate * value for rate, value in zip(rates, tangent)]
        if shift is not None:
            gap = [value - past for value, past in zip(gap, shift)]
        root = [jnp.sqrt(reaction_span * rate * (1.0 - value * value)) for rate, value in zip(rates, tangent)]
        matrix = {}
        for i in range(minerals):
            for j in range(i + 1):
                entry = root[i] * root[j] * powers[i, j]
                matrix[(i, j)] = entry + 1.0 if i == j else entry
        right = []
        for i in range(minerals):
            total = None
            for j in range(minerals):
                term = powers[i, j] * gap[j]
                total = term if total is None else total + term
            right.append(root[i] * total)
        inverse = [None] * minerals
        for j in range(minerals):
            inverse[j] = lax.rsqrt(matrix[(j, j)])
            for i in range(j + 1, minerals):
                matrix[(i, j)] = matrix[(i, j)] * inverse[j]
            right[j] = right[j] * inverse[j]
            for i in range(j + 1, minerals):
                right[i] = right[i] - matrix[(i, j)] * right[j]
                for k in range(j + 1, i + 1):
                    matrix[(i, k)] = matrix[(i, k)] - matrix[(i, j)] * matrix[(k, j)]
        for i in reversed(range(minerals)):
            right[i] = right[i] * inverse[i]
            for k in range(i):
                right[k] = right[k] - matrix[(i, k)] * right[i]
        delta = [newton_damping * (g - e * w) for g, e, w in zip(gap, root, right)]
        shift = delta if shift is None else [past + step for past, step in zip(shift, delta)]
    result = []
    for value, row in zip(moved, rows):
        for m in range(minerals):
            value = value - stoich[row, m] * shift[m]
        result.append(value)
    return result


def finish_kernel(groups, store_t, rate_t, stoich, powers, log_equil, stats, sums, mineral, basis, kx, ky, kz, above, below, *refs):
    count = lax.axis_size("sp")
    blocks, (head_out, *outs) = refs[:count], refs[count : 2 * count + 1]
    head_s, pair_s = refs[2 * count + 1 :]
    me = lax.axis_index("sp")
    layers, rows = head_out.shape[:2]
    tall, wide = head_s.shape[1:]

    total = jnp.sum(sums[...], axis=0, keepdims=True)
    lane = lane_ids(pair_s.shape)
    row = lax.broadcasted_iota(jnp.int32, pair_s.shape, 0)
    spread = jnp.sum(jnp.where(lane == row, total, 0.0), axis=1, keepdims=True)
    pair_s[...] = jnp.broadcast_to(spread, pair_s.shape)
    top = jnp.max(stats[...], axis=0, keepdims=True)
    low = store_t[0]
    for k in range(1, store_t.shape[0]):
        low = jnp.minimum(low, store_t[k])
    gram = [pair_s[at : at + 1, :] for at in range(len(PAIRS))]
    weights = direction_weights(gram, top / (4.0 * low))
    weights = [jnp.concatenate([w * (4.0 / top)] * (wide // LANES), axis=1) for w in weights]
    for z in range(layers):
        value = weights[0] * basis[0, z]
        for k in range(1, ITERS):
            value = value + weights[k] * basis[k, z]
        head_s[z] = value
        head_out[z] = value[rows : 2 * rows, :LANES]

    shape = (rows, LANES)
    lane = lane_ids(shape)
    row = lax.broadcasted_iota(jnp.int32, shape, 0)
    center = slice(rows, 2 * rows)

    def layer(z, carry):
        before, after = jnp.maximum(z - 1, 0), jnp.minimum(z + 1, layers - 1)
        value = head_s[z, :, :LANES]
        face = kx[z, :, :LANES]
        flow = face * (value - pltpu.roll(value, tall - 1, 0))
        faces = [(face[center], flow[center])]
        faces.append((pltpu.roll(face, 1, 0)[center], -pltpu.roll(flow, 1, 0)[center]))
        value = head_s[z, center, :]
        face = ky[z, center, :]
        flow = face * (value - pltpu.roll(value, wide - 1, 1))
        faces.append((face[:, :LANES], flow[:, :LANES]))
        faces.append((pltpu.roll(face, 1, 1)[:, :LANES], -pltpu.roll(flow, 1, 1)[:, :LANES]))
        value = value[:, :LANES]
        for face, other in ((kz[z + 1, center, :LANES], after), (kz[z, center, :LANES], before)):
            faces.append((face, face * (value - head_s[other, center, :LANES])))
        outward = None
        inward = []
        for face, flow in faces:
            term = jnp.maximum(flow, 0.0) + dispersion * face
            outward = term if outward is None else outward + term
            inward.append(time_step * (dispersion * face - jnp.minimum(flow, 0.0)))
        stay = 1.0 - time_step * outward

        moved, table_rows = [], []
        for d, block in enumerate(blocks):
            base = block.shape[0] - groups * layers - 1
            group = lax.rem(me + count - d, count)
            edge = block[base + groups * layers]
            for c in range(groups):
                at = base + c * layers
                here = block[at + z]
                side = pltpu.roll(edge, LANES - 1 - 2 * (c * layers + z), 1)
                line = pl.ds(z, 1)
                edge_at = 4 * layers + d * groups + c
                following = jnp.where(row == rows - 1, below[edge_at, line, :], pltpu.roll(here, rows - 1, 0))
                preceding = jnp.where(row == 0, above[edge_at, line, :], pltpu.roll(here, 1, 0))
                result = stay * here + inward[0] * following + inward[1] * preceding
                result = result + inward[2] * jnp.where(lane == LANES - 1, side, pltpu.roll(here, LANES - 1, 1))
                result = result + inward[3] * jnp.where(lane == 0, side, pltpu.roll(here, 1, 1))
                result = result + inward[4] * block[at + after] + inward[5] * block[at + before]
                moved.append(result)
                table_rows.append(group * groups + c)
        labels = mineral[z]
        rates = []
        for m in range(rate_t.shape[1]):
            rate = jnp.zeros(shape, jnp.float32)
            for level in range(rate_t.shape[0]):
                rate = jnp.where(labels == level, rate_t[level, m], rate)
            rates.append(rate)
        reacted = react(moved, rates, powers, stoich, table_rows, log_equil)
        for at, result in enumerate(reacted):
            outs[at // groups][(at % groups) * layers + z] = result
        return carry

    lax.fori_loop(0, layers, layer, 0)


def place_kernel(*refs):
    *blocks, out = refs
    count = len(blocks)
    me = lax.axis_index("sp")
    groups, layers = out.shape[:2]
    for d, block in enumerate(blocks):
        column = pl.multiple_of(lax.rem(me + d, count) * LANES, LANES)
        for c in range(groups):
            for z in range(layers):
                out[c, z, :, pl.ds(column, LANES)] = block[c * layers + z]


def call(kernel, tables, arrays, out_shapes, scratch=()):
    smem = pl.BlockSpec(memory_space=pltpu.SMEM)
    vmem = pl.BlockSpec(memory_space=pltpu.VMEM)
    shapes = [jax.ShapeDtypeStruct(shape, jnp.float32) for shape in out_shapes]
    return pl.pallas_call(
        kernel,
        out_shape=shapes,
        in_specs=[smem] * len(tables) + [vmem] * len(arrays),
        out_specs=[vmem] * len(shapes),
        scratch_shapes=[pltpu.VMEM(shape, jnp.float32) for shape in scratch],
    )(*tables, *arrays)


def shifted(array, axis, amount):
    count = lax.axis_size(axis)
    return lax.ppermute(array, axis, [(i, (i + amount) % count) for i in range(count)])


def per_device(
    previous_head,
    recharge,
    soil_zone,
    soil_cond,
    soil_store,
    species,
    mineral_zone,
    rate_table,
    stoich,
    log_equil,
):
    count = lax.axis_size("sp")
    devices = count * lax.axis_size("gx")
    layers, rows, columns = previous_head.shape
    groups = species.shape[0]
    assert columns == LANES and layers == 8 and rows == 8 and count > 2
    own_tiles = groups * layers + 1
    tile = (rows, LANES)

    tiles = [own_tiles + (2 * layers if d in (1, count - 1) else 0) for d in range(count)]
    *blocks, stats = call(
        pack_kernel,
        [soil_cond, soil_store],
        [previous_head, recharge, soil_zone, species],
        [(t,) + tile for t in tiles] + [(devices, LANES)],
    )
    field = blocks[1]
    blocks = [blocks[0]] + [shifted(blocks[d], "sp", d) for d in range(1, count)]
    stats = lax.all_to_all(stats, ("gx", "sp"), 0, 0, tiled=True)
    wide_tiles = 4 * layers + count * groups
    up, down = call(
        functools.partial(widen_kernel, groups), [], [field] + blocks, [(wide_tiles,) + tile] * 2
    )
    below, above = shifted(up, "gx", -1), shifted(down, "gx", 1)
    extended = (layers, 3 * rows, 2 * LANES)
    basis, kx, ky, kz, sums = call(
        krylov_kernel,
        [soil_cond, soil_store],
        [stats, up, above, below],
        [(BASIS,) + extended, extended, extended, (layers + 1,) + extended[1:], (devices, LANES)],
        [extended, extended, (PAIR_ROWS, LANES)],
    )
    sums = lax.all_to_all(sums, ("gx", "sp"), 0, 0, tiled=True)
    powers = jnp.dot(stoich.T, stoich, precision=lax.Precision.HIGHEST, preferred_element_type=jnp.float32)
    head_field, *reacted = call(
        functools.partial(finish_kernel, groups),
        [soil_store, rate_table, stoich, powers, log_equil],
        [stats, sums, mineral_zone, basis, kx, ky, kz, above, below] + blocks,
        [(layers,) + tile] + [(groups * layers,) + tile] * count,
        [extended, (PAIR_ROWS, LANES)],
    )
    reacted = [reacted[0]] + [shifted(reacted[d], "sp", -d) for d in range(1, count)]
    (species_out,) = call(place_kernel, [], reacted, [species.shape])
    return (head_field, species_out)


def solution(mesh):
    in_specs = (
        P(None, "gx", "sp"),
        P(None, "gx", "sp"),
        P(None, "gx", "sp"),
        P(),
        P(),
        P("sp", None, "gx", None),
        P(None, "gx", "sp"),
        P(),
        P(),
        P(),
    )
    out_specs = (P(None, "gx", "sp"), P("sp", None, "gx", None))
    return jax.shard_map(
        per_device, mesh=mesh, in_specs=in_specs, out_specs=out_specs, check_vma=False
    )
```

```python
import functools

import jax
import jax.numpy as jnp
from jax import lax
from jax.experimental import pallas as pl
from jax.experimental.pallas import tpu as pltpu
from jax.sharding import PartitionSpec as P


ITERS = 6
NEWTON = 2

time_step = 0.05
dispersion = 0.5
reaction_span = 0.5
newton_damping = 0.5

LANES = 128
VMEM_BYTES = 16 * 1024 * 1024
WHOLE_VMEM_BYTES = 60 * 1024 * 1024
BASIS = ITERS + 1
HALO = ITERS + 1
PAIRS = [(i, j) for j in range(BASIS) for i in range(j + 1)]
PAIR_AT = {pair: at for at, pair in enumerate(PAIRS)}
PAIR_ROWS = -(-len(PAIRS) // 8) * 8


def harmonic(center, other):
    return 2.0 * center * other / jnp.maximum(center + other, 1e-30)


def pick(labels, table, first):
    value = jnp.zeros(labels.shape, jnp.float32)
    for level in range(table.shape[0]):
        value = jnp.where(labels == level + first, table[level], value)
    return value


def lane_ids(shape):
    return lax.broadcasted_iota(jnp.int32, shape, len(shape) - 1)


def fetch(pairs, sems):
    copies = [pltpu.make_async_copy(source, target, sems.at[at]) for at, (source, target) in enumerate(pairs)]
    for copy in copies:
        copy.start()
    for copy in copies:
        copy.wait()


def field_kernel(cond_h, store_h, previous_h, recharge_h, zone_h, field, sides, cond_t, store_t, previous, recharge, zone, sems):
    fetch(
        [(cond_h, cond_t), (store_h, store_t), (previous_h, previous), (recharge_h, recharge), (zone_h, zone)],
        sems,
    )
    count = lax.axis_size("sp")
    me = lax.axis_index("sp")
    layers = previous.shape[0]
    shape = previous.shape[1:]
    lane = lane_ids(shape)
    conduct, bound = [], []
    to_left = to_right = jnp.zeros(shape, jnp.float32)
    for z in range(layers):
        labels = zone[z]
        conduct.append(pick(labels, cond_t, 0))
        storage = pick(labels, store_t, 0)
        bound.append(storage)
        values = (storage * previous[z] + recharge[z], (labels + 1).astype(jnp.float32))
        for part, value in enumerate(values):
            at = part * layers + z
            field[at] = value
            here = jnp.logical_and(lane >= at * HALO, lane < (at + 1) * HALO)
            to_left = jnp.where(here, pltpu.roll(value, at * HALO, 1), to_left)
            to_right = jnp.where(here, pltpu.roll(value, (at + 1) * HALO % LANES, 1), to_right)
    power = jnp.zeros(shape, jnp.float32)
    upright = [harmonic(conduct[z], conduct[(z + 1) % layers]) for z in range(layers)]
    for z in range(layers):
        here = conduct[z]
        total = upright[z] + upright[z - 1]
        for axis in range(2):
            face = harmonic(here, pltpu.roll(here, 1, axis))
            total = total + face + pltpu.roll(face, shape[axis] - 1, axis)
        square = bound[z] + 2.0 * total
        square = square * square
        power = power + square * square
    column = jnp.sum(power, axis=0, keepdims=True) * (1.0 / (layers * shape[0]))
    top = jnp.broadcast_to(jnp.max(column, axis=1, keepdims=True), shape)
    for s in range(count):
        tile = jnp.where(me + 1 == s, to_right, jnp.where(me - 1 == s, to_left, 0.0))
        tile = jnp.where(lane >= 2 * layers * HALO, top, tile)
        for g in range(sides.shape[0] // count):
            sides[g * count + s] = tile


def pack_kernel(species, *blocks):
    count = len(blocks)
    me = lax.axis_index("sp")
    groups, layers, rows = species.shape[:3]
    shape = (rows, LANES)
    lane = lane_ids(shape)
    for d in range(count):
        here = jnp.bitwise_xor(me, d)
        sides = (lax.rem(here + count - 1, count), here, lax.rem(here + 1, count))
        at = [pl.ds(pl.multiple_of(i * LANES, LANES), LANES) for i in sides]
        edge = jnp.zeros(shape, jnp.float32)
        for c in range(groups):
            for z in range(layers):
                j = c * layers + z
                blocks[d][j] = species[c, z, :, at[1]]
                edge = jnp.where(lane == 2 * j, pltpu.roll(species[c, z, :, at[2]], 2 * j, 1), edge)
                edge = jnp.where(
                    lane == 2 * j + 1, pltpu.roll(species[c, z, :, at[0]], 2 * j + 2, 1), edge
                )
        blocks[d][groups * layers] = edge


def rim_kernel(groups, *refs):
    *blocks, _, up, down = refs
    rows = blocks[0].shape[1]
    layers = (blocks[0].shape[0] - 1) // groups
    for d, block in enumerate(blocks):
        for c in range(groups):
            at = pl.ds(c * layers, layers)
            up[d * groups + c] = block[at, 0, :]
            down[d * groups + c] = block[at, rows - 1, :]


def krylov_kernel(cond_t, store_t, sides, previous, recharge, zone, above, below, basis, kx, ky, kz, scale, sums, cond_s, store_s, pair_s):
    tall_count, count = lax.axis_size("gx"), lax.axis_size("sp")
    me, me_s = lax.axis_index("gx"), lax.axis_index("sp")
    layers, tall, wide = cond_s.shape
    rows = tall // 3
    lane = lane_ids((rows, LANES))
    tops = jnp.max(sides[...], axis=0)
    tops = jnp.max(jnp.where(lane >= 2 * layers * HALO, tops, 0.0), axis=0, keepdims=True)
    top = jnp.sqrt(jnp.sqrt(jnp.max(tops, axis=1, keepdims=True)))
    scale[...] = jnp.broadcast_to(4.0 / top, scale.shape)
    twice = jnp.broadcast_to(2.0 / top, (1, wide))
    fourth = jnp.broadcast_to(4.0 / top, (1, wide))

    for part, block in enumerate((above, None, below)):
        there = me + part - 1
        valid = jnp.logical_and(there >= 0, there < tall_count)
        there = jnp.clip(there, 0, tall_count - 1) * count
        keep = valid.astype(jnp.float32)
        keep_left = jnp.logical_and(valid, me_s > 0).astype(jnp.float32)
        keep_right = jnp.logical_and(valid, me_s < count - 1).astype(jnp.float32)
        left = sides[there + jnp.maximum(me_s - 1, 0)] * keep_left
        right = sides[there + jnp.minimum(me_s + 1, count - 1)] * keep_right
        at = slice(part * rows, (part + 1) * rows)
        for z in range(layers):
            near = []
            for j in (z, layers + z):
                value = jnp.where(lane < HALO, pltpu.roll(right, (LANES - j * HALO) % LANES, 1), 0.0)
                value = jnp.where(
                    lane >= LANES - HALO, pltpu.roll(left, LANES - (j + 1) * HALO, 1), value
                )
                near.append(value)
            if block is None:
                field, labels = None, zone[z] + 1
            else:
                field, labels = block[z] * keep, block[layers + z] * keep
            for half, (field, labels) in enumerate(((field, labels), near)):
                cols = slice(half * LANES, (half + 1) * LANES)
                storage = pick(labels, store_t, 1)
                if field is None:
                    field = storage * previous[z] + recharge[z]
                basis[0, z, at, cols] = field
                cond_s[z, at, cols] = pick(labels, cond_t, 1)
                store_s[z, at, cols] = storage
    kz[0] = jnp.zeros((tall, wide), jnp.float32)
    for z in range(layers):
        here = cond_s[z]
        kx[z] = harmonic(here, pltpu.roll(here, tall - 1, 0))
        ky[z] = harmonic(here, pltpu.roll(here, wide - 1, 1))
        if z + 1 < layers:
            kz[z + 1] = harmonic(here, cond_s[z + 1])

    def operate(k):
        flow = None
        for z in range(layers):
            value = basis[k, z]
            along_x = kx[z] * (value - pltpu.roll(value, tall - 1, 0))
            along_y = ky[z] * (value - pltpu.roll(value, wide - 1, 1))
            image = store_s[z] * value
            image = image + (along_x - pltpu.roll(along_x, 1, 0))
            image = image + (along_y - pltpu.roll(along_y, 1, 1))
            if z + 1 < layers:
                along_z = kz[z + 1] * (value - basis[k, z + 1])
                image = image + along_z
            if z:
                image = image - flow
            flow = along_z
            yield z, value, image

    for z, value, image in operate(0):
        basis[1, z] = image * twice - value

    def step(k, carry):
        for z, value, image in operate(k):
            basis[k + 1, z] = image * fourth - 2.0 * value - basis[k - 1, z]
        return carry

    lax.fori_loop(1, ITERS, step, 0)

    totals = [None] * len(PAIRS)
    for z in range(layers):
        values = [basis[k, z, rows : 2 * rows, :LANES] for k in range(BASIS)]
        for at, (i, j) in enumerate(PAIRS):
            term = values[i] * values[j]
            totals[at] = term if z == 0 else totals[at] + term
    pair_s[...] = jnp.zeros(pair_s.shape, jnp.float32)
    for at, total in enumerate(totals):
        pair_s[at : at + 1, :] = jnp.sum(total, axis=0, keepdims=True)
    full = jnp.sum(pair_s[...], axis=1, keepdims=True)
    lane = lane_ids(pair_s.shape)
    row = lax.broadcasted_iota(jnp.int32, pair_s.shape, 0)
    line = jnp.sum(jnp.where(lane == row, full, 0.0), axis=0, keepdims=True)
    sums[...] = jnp.broadcast_to(line, sums.shape)


def galerkin_weights(gram):
    def inner(i, j):
        return gram[PAIR_AT[(min(i, j), max(i, j))]]

    matrix = {}
    for i in range(ITERS):
        for j in range(i + 1):
            if j == 0:
                matrix[(i, j)] = 2.0 * (inner(i, 0) + inner(i, 1))
            else:
                matrix[(i, j)] = inner(i, j + 1) + inner(i, j - 1) + 2.0 * inner(i, j)
    least = [matrix[(i, i)] * 2e-7 for i in range(ITERS)]
    right = [inner(i, 0) for i in range(ITERS)]
    inverse = []
    for j in range(ITERS):
        pivot = matrix[(j, j)]
        good = pivot > least[j]
        inverse.append(jnp.where(good, 1.0 / jnp.where(good, pivot, 1.0), 0.0))
        for i in range(j + 1, ITERS):
            factor = matrix[(i, j)] * inverse[j]
            right[i] = right[i] - factor * right[j]
            for k in range(j + 1, i + 1):
                matrix[(i, k)] = matrix[(i, k)] - factor * matrix[(k, j)]
    for i in reversed(range(ITERS)):
        for k in range(i + 1, ITERS):
            right[i] = right[i] - matrix[(k, i)] * right[k]
        right[i] = right[i] * inverse[i]
    return right


def react(moved, rates, powers, stoich, rows, log_equil):
    minerals = len(rates)
    first = []
    for m in range(minerals):
        total = None
        for value, row in zip(moved, rows):
            term = stoich[row, m] * value
            total = term if total is None else total + term
        first.append(total - log_equil[m])
    shift = None
    for _ in range(NEWTON):
        if shift is None:
            affinity = first
        else:
            affinity = []
            for m in range(minerals):
                total = first[m]
                for n in range(minerals):
                    total = total - powers[m, n] * shift[n]
                affinity.append(total)
        tangent = [jnp.tanh(value) for value in affinity]
        gap = [reaction_span * rate * value for rate, value in zip(rates, tangent)]
        if shift is not None:
            gap = [value - past for value, past in zip(gap, shift)]
        root = [jnp.sqrt(reaction_span * rate * (1.0 - value * value)) for rate, value in zip(rates, tangent)]
        matrix = {}
        for i in range(minerals):
            for j in range(i + 1):
                entry = root[i] * root[j] * powers[i, j]
                matrix[(i, j)] = entry + 1.0 if i == j else entry
        right = []
        for i in range(minerals):
            total = None
            for j in range(minerals):
                term = powers[i, j] * gap[j]
                total = term if total is None else total + term
            right.append(root[i] * total)
        inverse = [None] * minerals
        for j in range(minerals):
            inverse[j] = lax.rsqrt(matrix[(j, j)])
            for i in range(j + 1, minerals):
                matrix[(i, j)] = matrix[(i, j)] * inverse[j]
            right[j] = right[j] * inverse[j]
            for i in range(j + 1, minerals):
                right[i] = right[i] - matrix[(i, j)] * right[j]
                for k in range(j + 1, i + 1):
                    matrix[(i, k)] = matrix[(i, k)] - matrix[(i, j)] * matrix[(k, j)]
        for i in reversed(range(minerals)):
            right[i] = right[i] * inverse[i]
            for k in range(i):
                right[k] = right[k] - matrix[(i, k)] * right[i]
        delta = [newton_damping * (g - e * w) for g, e, w in zip(gap, root, right)]
        shift = delta if shift is None else [past + step for past, step in zip(shift, delta)]
    result = []
    for value, row in zip(moved, rows):
        for m in range(minerals):
            value = value - stoich[row, m] * shift[m]
        result.append(value)
    return result


def finish_kernel(groups, rate_t, stoich, powers, log_equil, scale, sums, mineral, basis, kx, ky, kz, above, below, *refs):
    count = lax.axis_size("sp")
    blocks, (head_out, *outs, head_s, pair_s) = refs[:count], refs[count:]
    me = lax.axis_index("sp")
    layers, rows = head_out.shape[:2]
    tall, wide = head_s.shape[1:]

    total = jnp.sum(sums[...], axis=0, keepdims=True)
    lane = lane_ids(pair_s.shape)
    row = lax.broadcasted_iota(jnp.int32, pair_s.shape, 0)
    spread = jnp.sum(jnp.where(lane == row, total, 0.0), axis=1, keepdims=True)
    pair_s[...] = jnp.broadcast_to(spread, pair_s.shape)
    gram = [pair_s[at : at + 1, :] for at in range(len(PAIRS))]
    weights = [weight * scale[0:1, :] for weight in galerkin_weights(gram)]
    weights = [jnp.concatenate([weight] * (wide // LANES), axis=1) for weight in weights]
    for z in range(layers):
        value = weights[0] * basis[0, z]
        for k in range(1, ITERS):
            value = value + weights[k] * basis[k, z]
        head_s[z] = value
        head_out[z] = value[rows : 2 * rows, :LANES]

    shape = (rows, LANES)
    lane = lane_ids(shape)
    row = lax.broadcasted_iota(jnp.int32, shape, 0)
    center = slice(rows, 2 * rows)

    def layer(z, carry):
        before, after = jnp.maximum(z - 1, 0), jnp.minimum(z + 1, layers - 1)
        value = head_s[z, :, :LANES]
        face = kx[z, :, :LANES]
        flow = face * (value - pltpu.roll(value, tall - 1, 0))
        faces = [(face[center], flow[center])]
        faces.append((pltpu.roll(face, 1, 0)[center], -pltpu.roll(flow, 1, 0)[center]))
        value = head_s[z, center, :]
        face = ky[z, center, :]
        flow = face * (value - pltpu.roll(value, wide - 1, 1))
        faces.append((face[:, :LANES], flow[:, :LANES]))
        faces.append((pltpu.roll(face, 1, 1)[:, :LANES], -pltpu.roll(flow, 1, 1)[:, :LANES]))
        value = value[:, :LANES]
        for face, other in ((kz[z + 1, center, :LANES], after), (kz[z, center, :LANES], before)):
            faces.append((face, face * (value - head_s[other, center, :LANES])))
        outward = None
        inward = []
        for face, flow in faces:
            term = jnp.maximum(flow, 0.0) + dispersion * face
            outward = term if outward is None else outward + term
            inward.append(time_step * (dispersion * face - jnp.minimum(flow, 0.0)))
        stay = 1.0 - time_step * outward

        moved, table_rows = [], []
        for d, block in enumerate(blocks):
            group = jnp.bitwise_xor(me, d)
            edge = block[groups * layers]
            for c in range(groups):
                at = c * layers
                here = block[at + z]
                side = pltpu.roll(edge, LANES - 1 - 2 * (c * layers + z), 1)
                line = pl.ds(z, 1)
                edge_at = d * groups + c
                following = jnp.where(row == rows - 1, below[edge_at, line, :], pltpu.roll(here, rows - 1, 0))
                preceding = jnp.where(row == 0, above[edge_at, line, :], pltpu.roll(here, 1, 0))
                result = stay * here + inward[0] * following + inward[1] * preceding
                result = result + inward[2] * jnp.where(lane == LANES - 1, side, pltpu.roll(here, LANES - 1, 1))
                result = result + inward[3] * jnp.where(lane == 0, side, pltpu.roll(here, 1, 1))
                result = result + inward[4] * block[at + after] + inward[5] * block[at + before]
                moved.append(result)
                table_rows.append(group * groups + c)
        labels = mineral[z]
        rates = []
        for m in range(rate_t.shape[1]):
            rate = jnp.zeros(shape, jnp.float32)
            for level in range(rate_t.shape[0]):
                rate = jnp.where(labels == level, rate_t[level, m], rate)
            rates.append(rate)
        reacted = react(moved, rates, powers, stoich, table_rows, log_equil)
        for at, result in enumerate(reacted):
            outs[at // groups][(at % groups) * layers + z] = result
        return carry

    lax.fori_loop(0, layers, layer, 0)


def place_kernel(*refs):
    *blocks, out = refs
    me = lax.axis_index("sp")
    groups, layers = out.shape[:2]
    for d, block in enumerate(blocks):
        column = pl.multiple_of(jnp.bitwise_xor(me, d) * LANES, LANES)
        for c in range(groups):
            for z in range(layers):
                out[c, z, :, pl.ds(column, LANES)] = block[c * layers + z]


def call(kernel, tables, arrays, out_shapes, scratch=(), space=pltpu.VMEM, limit=VMEM_BYTES):
    smem = pl.BlockSpec(memory_space=pltpu.SMEM)
    vmem = pl.BlockSpec(memory_space=pltpu.VMEM)
    outside = pl.BlockSpec(memory_space=space)
    shapes = [jax.ShapeDtypeStruct(shape, jnp.float32) for shape in out_shapes]
    return pl.pallas_call(
        kernel,
        out_shape=shapes,
        in_specs=[smem] * len(tables) + [outside] * len(arrays),
        out_specs=[vmem] * len(shapes),
        scratch_shapes=[pltpu.VMEM(one, jnp.float32) if isinstance(one, tuple) else one for one in scratch],
        compiler_params=pltpu.CompilerParams(vmem_limit_bytes=limit),
        cost_estimate=pl.CostEstimate(flops=200_000_000, bytes_accessed=4_000_000, transcendentals=0),
    )(*tables, *arrays)


def shifted(array, axis, amount):
    count = lax.axis_size(axis)
    return lax.ppermute(array, axis, [(i, (i + amount) % count) for i in range(count)])


def swapped(array, axis, mask):
    count = lax.axis_size(axis)
    return lax.ppermute(array, axis, [(i, i ^ mask) for i in range(count)])


def per_device(
    previous_head,
    recharge,
    soil_zone,
    soil_cond,
    soil_store,
    species,
    mineral_zone,
    rate_table,
    stoich,
    log_equil,
):
    count = lax.axis_size("sp")
    devices = count * lax.axis_size("gx")
    layers, rows, columns = previous_head.shape
    groups = species.shape[0]
    assert columns == LANES and layers == 8 and rows == 8 and count & (count - 1) == 0
    assert 2 * layers * HALO < LANES and 2 * groups * layers <= LANES
    tile = (rows, LANES)
    everywhere = ("gx", "sp")

    field, sides = call(
        field_kernel,
        [],
        [soil_cond, soil_store, previous_head, recharge, soil_zone],
        [(2 * layers,) + tile, (devices,) + tile],
        [pltpu.SMEM(soil_cond.shape, jnp.float32), pltpu.SMEM(soil_store.shape, jnp.float32)]
        + [(layers,) + tile] * 2
        + [pltpu.VMEM((layers,) + tile, jnp.int32), pltpu.SemaphoreType.DMA((5,))],
        pltpu.HBM,
        WHOLE_VMEM_BYTES,
    )
    sides = lax.all_to_all(sides, everywhere, 0, 0, tiled=True)
    below = shifted(field, "gx", -1)
    above = shifted(field, "gx", 1)
    blocks = call(pack_kernel, [], [species], [(groups * layers + 1,) + tile] * count)
    arrived = {d: swapped(blocks[d], "sp", d) for d in range(count - 1, 0, -1)}
    blocks = [blocks[0]] + [arrived[d] for d in range(1, count)]
    extended = (layers, 3 * rows, 2 * LANES)
    basis, kx, ky, kz, scale, sums = call(
        krylov_kernel,
        [soil_cond, soil_store],
        [sides, previous_head, recharge, soil_zone, above, below],
        [(BASIS,) + extended, extended, extended, (layers + 1,) + extended[1:], tile, (devices, LANES)],
        [extended, extended, (PAIR_ROWS, LANES)],
    )
    sums = lax.all_to_all(sums, everywhere, 0, 0, tiled=True)
    rims = call(
        functools.partial(rim_kernel, groups), [], blocks + [scale], [(count * groups, layers, LANES)] * 2
    )
    below, above = shifted(rims[0], "gx", -1), shifted(rims[1], "gx", 1)
    powers = jnp.dot(stoich.T, stoich, precision=lax.Precision.HIGHEST, preferred_element_type=jnp.float32)
    head_field, *reacted = call(
        functools.partial(finish_kernel, groups),
        [rate_table, stoich, powers, log_equil],
        [scale, sums, mineral_zone, basis, kx, ky, kz, above, below] + blocks,
        [(layers,) + tile] + [(groups * layers,) + tile] * count,
        [extended, (PAIR_ROWS, LANES)],
    )
    arrived = {d: swapped(reacted[d], "sp", d) for d in range(count - 1, 0, -1)}
    (species_out,) = call(place_kernel, [], [reacted[0]] + [arrived[d] for d in range(1, count)], [species.shape])
    return (head_field, species_out)


def solution(mesh):
    in_specs = (
        P(None, "gx", "sp"),
        P(None, "gx", "sp"),
        P(None, "gx", "sp"),
        P(),
        P(),
        P("sp", None, "gx", None),
        P(None, "gx", "sp"),
        P(),
        P(),
        P(),
    )
    out_specs = (P(None, "gx", "sp"), P("sp", None, "gx", None))

    return jax.shard_map(per_device, mesh=mesh, in_specs=in_specs, out_specs=out_specs, check_vma=False)
```

```python
import functools

import jax
import jax.numpy as jnp
from jax import lax
from jax.experimental import pallas as pl
from jax.experimental.pallas import tpu as pltpu
from jax.sharding import PartitionSpec as P


ITERS = 6
NEWTON = 2

time_step = 0.05
dispersion = 0.5
reaction_span = 0.5
newton_damping = 0.5

LANES = 128
VMEM_BYTES = 16 * 1024 * 1024
WHOLE_VMEM_BYTES = 60 * 1024 * 1024
BASIS = ITERS + 1
HALO = ITERS + 1
LAYERS_TOGETHER = 4
PAIRS = [(i, j) for j in range(BASIS) for i in range(j + 1)]
PAIR_AT = {pair: at for at, pair in enumerate(PAIRS)}
PAIR_ROWS = -(-len(PAIRS) // 8) * 8


def harmonic(center, other):
    return 2.0 * center * other / jnp.maximum(center + other, 1e-30)


def pick(labels, table, first):
    value = jnp.zeros(labels.shape, jnp.float32)
    for level in range(table.shape[0]):
        value = jnp.where(labels == level + first, table[level], value)
    return value


def lane_ids(shape):
    return lax.broadcasted_iota(jnp.int32, shape, len(shape) - 1)


def fetch(pairs, sems, later):
    copies = [
        pltpu.make_async_copy(source, target, sems.at[at]) for at, (source, target) in enumerate(pairs + later)
    ]
    for copy in copies:
        copy.start()
    for copy in copies[: len(pairs)]:
        copy.wait()
    return copies[len(pairs) :]


def field_kernel(cond_h, store_h, previous_h, recharge_h, zone_h, species_h, field, sides, *refs):
    *blocks, cond_t, store_t, previous, recharge, zone, species, sems = refs
    (species_copy,) = fetch(
        [(cond_h, cond_t), (store_h, store_t), (previous_h, previous), (recharge_h, recharge), (zone_h, zone)],
        sems,
        [(species_h, species)],
    )
    count = lax.axis_size("sp")
    me = lax.axis_index("sp")
    layers = previous.shape[0]
    shape = previous.shape[1:]
    lane = lane_ids(shape)
    conduct, bound = [], []
    to_left = to_right = jnp.zeros(shape, jnp.float32)
    for z in range(layers):
        labels = zone[z]
        conduct.append(pick(labels, cond_t, 0))
        storage = pick(labels, store_t, 0)
        bound.append(storage)
        values = (storage * previous[z] + recharge[z], (labels + 1).astype(jnp.float32))
        for part, value in enumerate(values):
            at = part * layers + z
            field[at] = value
            here = jnp.logical_and(lane >= at * HALO, lane < (at + 1) * HALO)
            to_left = jnp.where(here, pltpu.roll(value, at * HALO, 1), to_left)
            to_right = jnp.where(here, pltpu.roll(value, (at + 1) * HALO % LANES, 1), to_right)
    power = jnp.zeros(shape, jnp.float32)
    upright = [harmonic(conduct[z], conduct[(z + 1) % layers]) for z in range(layers)]
    for z in range(layers):
        here = conduct[z]
        total = upright[z] + upright[z - 1]
        for axis in range(2):
            face = harmonic(here, pltpu.roll(here, 1, axis))
            total = total + face + pltpu.roll(face, shape[axis] - 1, axis)
        square = bound[z] + 2.0 * total
        square = square * square
        power = power + square * square
    column = jnp.sum(power, axis=0, keepdims=True) * (1.0 / (layers * shape[0]))
    top = jnp.broadcast_to(jnp.max(column, axis=1, keepdims=True), shape)
    for s in range(count):
        tile = jnp.where(me + 1 == s, to_right, jnp.where(me - 1 == s, to_left, 0.0))
        tile = jnp.where(lane >= 2 * layers * HALO, top, tile)
        for g in range(sides.shape[0] // count):
            sides[g * count + s] = tile
    species_copy.wait()
    pack(species, *blocks)


def pack(species, *blocks):
    count = len(blocks)
    me = lax.axis_index("sp")
    groups, layers, rows = species.shape[:3]
    shape = (rows, LANES)
    lane = lane_ids(shape)
    for d in range(count):
        here = jnp.bitwise_xor(me, d)
        sides = (lax.rem(here + count - 1, count), here, lax.rem(here + 1, count))
        at = [pl.ds(pl.multiple_of(i * LANES, LANES), LANES) for i in sides]
        edge = jnp.zeros(shape, jnp.float32)
        for c in range(groups):
            for z in range(layers):
                j = c * layers + z
                blocks[d][j] = species[c, z, :, at[1]]
                edge = jnp.where(lane == 2 * j, pltpu.roll(species[c, z, :, at[2]], 2 * j, 1), edge)
                edge = jnp.where(
                    lane == 2 * j + 1, pltpu.roll(species[c, z, :, at[0]], 2 * j + 2, 1), edge
                )
        blocks[d][groups * layers] = edge


def rim_kernel(groups, *refs):
    *blocks, _, up, down = refs
    rows = blocks[0].shape[1]
    layers = (blocks[0].shape[0] - 1) // groups
    for d, block in enumerate(blocks):
        for c in range(groups):
            at = pl.ds(c * layers, layers)
            up[d * groups + c] = block[at, 0, :]
            down[d * groups + c] = block[at, rows - 1, :]


def rates_kernel(rate_t, mineral, half_rates):
    layers = mineral.shape[0]
    for z in range(layers):
        labels = mineral[z]
        masks = [labels == level for level in range(rate_t.shape[0])]
        for m in range(rate_t.shape[1]):
            rate = jnp.zeros(labels.shape, jnp.float32)
            for level, mask in enumerate(masks):
                rate = jnp.where(mask, reaction_span * rate_t[level, m], rate)
            half_rates[m * layers + z] = rate


def powers_kernel(stoich, powers, products):
    values = stoich[...]
    result = lax.dot_general(
        values,
        values,
        (((0,), (0,)), ((), ())),
        precision=lax.Precision.HIGHEST,
        preferred_element_type=jnp.float32,
    )
    powers[...] = result
    products[...] = result[:, :1] * result[:1, :]


def krylov_kernel(cond_t, store_t, sides, previous, recharge, zone, above, below, basis, kx, ky, kz, scale, sums, cond_s, store_s, pair_s):
    tall_count, count = lax.axis_size("gx"), lax.axis_size("sp")
    me, me_s = lax.axis_index("gx"), lax.axis_index("sp")
    layers, tall, wide = cond_s.shape
    rows = tall // 3
    lane = lane_ids((rows, LANES))
    tops = jnp.max(sides[...], axis=0)
    tops = jnp.max(jnp.where(lane >= 2 * layers * HALO, tops, 0.0), axis=0, keepdims=True)
    top = jnp.sqrt(jnp.sqrt(jnp.max(tops, axis=1, keepdims=True)))
    scale[...] = jnp.broadcast_to(4.0 / top, scale.shape)
    twice = jnp.broadcast_to(2.0 / top, (1, wide))
    fourth = jnp.broadcast_to(4.0 / top, (1, wide))

    for part, block in enumerate((above, None, below)):
        there = me + part - 1
        valid = jnp.logical_and(there >= 0, there < tall_count)
        there = jnp.clip(there, 0, tall_count - 1) * count
        keep = valid.astype(jnp.float32)
        keep_left = jnp.logical_and(valid, me_s > 0).astype(jnp.float32)
        keep_right = jnp.logical_and(valid, me_s < count - 1).astype(jnp.float32)
        left = sides[there + jnp.maximum(me_s - 1, 0)] * keep_left
        right = sides[there + jnp.minimum(me_s + 1, count - 1)] * keep_right
        at = slice(part * rows, (part + 1) * rows)
        for z in range(layers):
            near = []
            for j in (z, layers + z):
                value = jnp.where(lane < HALO, pltpu.roll(right, (LANES - j * HALO) % LANES, 1), 0.0)
                value = jnp.where(
                    lane >= LANES - HALO, pltpu.roll(left, LANES - (j + 1) * HALO, 1), value
                )
                near.append(value)
            if block is None:
                field, labels = None, zone[z] + 1
            else:
                field, labels = block[z] * keep, block[layers + z] * keep
            for half, (field, labels) in enumerate(((field, labels), near)):
                cols = slice(half * LANES, (half + 1) * LANES)
                storage = pick(labels, store_t, 1)
                if field is None:
                    field = storage * previous[z] + recharge[z]
                basis[0, z, at, cols] = field
                cond_s[z, at, cols] = pick(labels, cond_t, 1)
                store_s[z, at, cols] = storage
    kz[0] = jnp.zeros((tall, wide), jnp.float32)
    for z in range(layers):
        here = cond_s[z]
        kx[z] = harmonic(here, pltpu.roll(here, tall - 1, 0))
        ky[z] = harmonic(here, pltpu.roll(here, wide - 1, 1))
        if z + 1 < layers:
            kz[z + 1] = harmonic(here, cond_s[z + 1])

    def operate(k):
        flow = None
        for z in range(layers):
            value = basis[k, z]
            along_x = kx[z] * (value - pltpu.roll(value, tall - 1, 0))
            along_y = ky[z] * (value - pltpu.roll(value, wide - 1, 1))
            image = store_s[z] * value
            image = image + (along_x - pltpu.roll(along_x, 1, 0))
            image = image + (along_y - pltpu.roll(along_y, 1, 1))
            if z + 1 < layers:
                along_z = kz[z + 1] * (value - basis[k, z + 1])
                image = image + along_z
            if z:
                image = image - flow
            flow = along_z
            yield z, value, image

    for z, value, image in operate(0):
        basis[1, z] = image * twice - value

    def step(k, carry):
        for z, value, image in operate(k):
            basis[k + 1, z] = image * fourth - 2.0 * value - basis[k - 1, z]
        return carry

    lax.fori_loop(1, ITERS, step, 0)

    totals = [None] * len(PAIRS)
    for z in range(layers):
        values = [basis[k, z, rows : 2 * rows, :LANES] for k in range(BASIS)]
        for at, (i, j) in enumerate(PAIRS):
            term = values[i] * values[j]
            totals[at] = term if z == 0 else totals[at] + term
    pair_s[...] = jnp.zeros(pair_s.shape, jnp.float32)
    for at, total in enumerate(totals):
        pair_s[at : at + 1, :] = jnp.sum(total, axis=0, keepdims=True)
    full = jnp.sum(pair_s[...], axis=1, keepdims=True)
    lane = lane_ids(pair_s.shape)
    row = lax.broadcasted_iota(jnp.int32, pair_s.shape, 0)
    line = jnp.sum(jnp.where(lane == row, full, 0.0), axis=0, keepdims=True)
    sums[...] = jnp.broadcast_to(line, sums.shape)


def galerkin_weights(gram):
    def inner(i, j):
        return gram[PAIR_AT[(min(i, j), max(i, j))]]

    matrix = {}
    for i in range(ITERS):
        for j in range(i + 1):
            if j == 0:
                matrix[(i, j)] = 2.0 * (inner(i, 0) + inner(i, 1))
            else:
                matrix[(i, j)] = inner(i, j + 1) + inner(i, j - 1) + 2.0 * inner(i, j)
    least = [matrix[(i, i)] * 2e-7 for i in range(ITERS)]
    right = [inner(i, 0) for i in range(ITERS)]
    inverse = []
    for j in range(ITERS):
        pivot = matrix[(j, j)]
        good = pivot > least[j]
        inverse.append(jnp.where(good, 1.0 / jnp.where(good, pivot, 1.0), 0.0))
        for i in range(j + 1, ITERS):
            factor = matrix[(i, j)] * inverse[j]
            right[i] = right[i] - factor * right[j]
            for k in range(j + 1, i + 1):
                matrix[(i, k)] = matrix[(i, k)] - factor * matrix[(k, j)]
    for i in reversed(range(ITERS)):
        for k in range(i + 1, ITERS):
            right[i] = right[i] - matrix[(k, i)] * right[k]
        right[i] = right[i] * inverse[i]
    return right


def react(moved, half_rates, powers, products, stoich, rows, log_equil):
    minerals = len(half_rates)
    first = []
    for m in range(minerals):
        total = None
        for value, row in zip(moved, rows):
            term = stoich[row, m] * value
            total = term if total is None else total + term
        first.append(total - log_equil[m])
    shift = None
    for newton_pass in range(NEWTON):
        affinity = first
        if shift is not None:
            affinity = [value - newton_damping * past for value, past in zip(first, image)]
        tangent = [jnp.tanh(value) for value in affinity]
        gap = [rate * value for rate, value in zip(half_rates, tangent)]
        if shift is not None:
            gap = [value - past for value, past in zip(gap, shift)]
        weight = [rate * (1.0 - value * value) for rate, value in zip(half_rates, tangent)]
        matrix = {(i, j): powers[i, j] for i in range(minerals) for j in range(i + 1)}
        inverse, ahead, drawn = [], [], [None] * minerals
        for k in range(minerals):
            scaled = 1.0 / (1.0 + weight[k] * matrix[(k, k)])
            inverse.append(scaled)
            left = gap[k] if k == 0 else gap[k] - weight[k] * drawn[k]
            ahead.append(left * scaled)
            factor = weight[k] * scaled
            for i in range(k + 1, minerals):
                term = matrix[(i, k)] * ahead[k]
                drawn[i] = term if k == 0 else drawn[i] + term
            for i in range(k + 1, minerals):
                if k == 0:
                    for j in range(1, i + 1):
                        matrix[(i, j)] = powers[i, j] - products[i, j] * factor
                else:
                    part = matrix[(i, k)] * factor
                    for j in range(k + 1, i + 1):
                        matrix[(i, j)] = matrix[(i, j)] - part * matrix[(j, k)]
        step, image = [None] * minerals, [None] * minerals
        for k in reversed(range(minerals)):
            total = None
            for j in range(k + 1, minerals):
                term = matrix[(j, k)] * step[j]
                total = term if total is None else total + term
            step[k] = ahead[k] if total is None else ahead[k] - weight[k] * inverse[k] * total
            if newton_pass + 1 < NEWTON:
                parts = [part for part in (drawn[k], total) if part is not None]
                image[k] = sum(parts, matrix[(k, k)] * step[k])
        delta = [newton_damping * value for value in step]
        shift = delta if shift is None else [past + value for past, value in zip(shift, delta)]
    result = []
    for value, row in zip(moved, rows):
        for m in range(minerals):
            value = value - stoich[row, m] * shift[m]
        result.append(value)
    return result


def finish_kernel(groups, stoich, powers, products, log_equil, scale, sums, half_rates, basis, kx, ky, kz, above, below, *refs):
    count = lax.axis_size("sp")
    blocks, (head_out, *outs, head_s, pair_s) = refs[:count], refs[count:]
    me = lax.axis_index("sp")
    layers, rows = head_out.shape[:2]
    tall, wide = head_s.shape[1:]

    total = jnp.sum(sums[...], axis=0, keepdims=True)
    lane = lane_ids(pair_s.shape)
    row = lax.broadcasted_iota(jnp.int32, pair_s.shape, 0)
    spread = jnp.sum(jnp.where(lane == row, total, 0.0), axis=1, keepdims=True)
    pair_s[...] = jnp.broadcast_to(spread, pair_s.shape)
    gram = [pair_s[at : at + 1, :] for at in range(len(PAIRS))]
    weights = [weight * scale[0:1, :] for weight in galerkin_weights(gram)]
    weights = [jnp.concatenate([weight] * (wide // LANES), axis=1) for weight in weights]
    for z in range(layers):
        value = weights[0] * basis[0, z]
        for k in range(1, ITERS):
            value = value + weights[k] * basis[k, z]
        head_s[z] = value
        head_out[z] = value[rows : 2 * rows, :LANES]

    together = LAYERS_TOGETHER
    shape = (together, rows, LANES)
    lane = lane_ids(shape)
    row = lax.broadcasted_iota(jnp.int32, shape, 1)
    center = slice(rows, 2 * rows)

    def layer(step, carry):
        z = step * together
        here_at = pl.ds(z, together)
        before, after = jnp.maximum(z - 1, 0), jnp.minimum(z + together, layers - 1)

        def beside(ref, base, here):
            first, last = ref[pl.ds(base + before, 1)], ref[pl.ds(base + after, 1)]
            return jnp.concatenate([here[1:], last], axis=0), jnp.concatenate([first, here[:-1]], axis=0)

        value = head_s[here_at, :, :LANES]
        face = kx[here_at, :, :LANES]
        flow = face * (value - pltpu.roll(value, tall - 1, 1))
        faces = [(face[:, center], flow[:, center])]
        faces.append((pltpu.roll(face, 1, 1)[:, center], -pltpu.roll(flow, 1, 1)[:, center]))
        value = head_s[here_at, center, :]
        face = ky[here_at, center, :]
        flow = face * (value - pltpu.roll(value, wide - 1, 2))
        faces.append((face[:, :, :LANES], flow[:, :, :LANES]))
        faces.append((pltpu.roll(face, 1, 2)[:, :, :LANES], -pltpu.roll(flow, 1, 2)[:, :, :LANES]))
        value = value[:, :, :LANES]
        heads = beside(head_s.at[:, center, :LANES], 0, value)
        for shift, other in zip((1, 0), heads):
            face = kz[pl.ds(z + shift, together), center, :LANES]
            faces.append((face, face * (value - other)))
        outward = None
        inward = []
        for face, flow in faces:
            term = jnp.maximum(flow, 0.0) + dispersion * face
            outward = term if outward is None else outward + term
            inward.append(time_step * (dispersion * face - jnp.minimum(flow, 0.0)))
        stay = 1.0 - time_step * outward

        moved, table_rows = [], []
        for d, block in enumerate(blocks):
            group = jnp.bitwise_xor(me, d)
            edge = block[groups * layers]
            for c in range(groups):
                at = c * layers
                here = block[pl.ds(at + z, together)]
                side = jnp.stack([pltpu.roll(edge, LANES - 1 - 2 * (at + z + u), 1) for u in range(together)])
                edge_at = d * groups + c
                lines = [ref[edge_at, here_at, :][:, None, :] for ref in (below, above)]
                following = jnp.where(row == rows - 1, lines[0], pltpu.roll(here, rows - 1, 1))
                preceding = jnp.where(row == 0, lines[1], pltpu.roll(here, 1, 1))
                result = stay * here + inward[0] * following + inward[1] * preceding
                result = result + inward[2] * jnp.where(lane == LANES - 1, side, pltpu.roll(here, LANES - 1, 2))
                result = result + inward[3] * jnp.where(lane == 0, side, pltpu.roll(here, 1, 2))
                over, under = beside(block, at, here)
                moved.append(result + inward[4] * over + inward[5] * under)
                table_rows.append(group * groups + c)
        rates = [half_rates[pl.ds(m * layers + z, together)] for m in range(half_rates.shape[0] // layers)]
        reacted = react(moved, rates, powers, products, stoich, table_rows, log_equil)
        for at, result in enumerate(reacted):
            outs[at // groups][pl.ds((at % groups) * layers + z, together)] = result
        return carry

    lax.fori_loop(0, layers // together, layer, 0)


def place_kernel(*refs):
    *blocks, out = refs
    me = lax.axis_index("sp")
    groups, layers = out.shape[:2]
    for d, block in enumerate(blocks):
        column = pl.multiple_of(jnp.bitwise_xor(me, d) * LANES, LANES)
        for c in range(groups):
            for z in range(layers):
                out[c, z, :, pl.ds(column, LANES)] = block[c * layers + z]


def call(kernel, tables, arrays, out_shapes, scratch=(), space=pltpu.VMEM, limit=VMEM_BYTES):
    smem = pl.BlockSpec(memory_space=pltpu.SMEM)
    vmem = pl.BlockSpec(memory_space=pltpu.VMEM)
    outside = pl.BlockSpec(memory_space=space)
    shapes = [jax.ShapeDtypeStruct(shape, jnp.float32) for shape in out_shapes]
    return pl.pallas_call(
        kernel,
        out_shape=shapes,
        in_specs=[smem] * len(tables) + [outside] * len(arrays),
        out_specs=[vmem] * len(shapes),
        scratch_shapes=[pltpu.VMEM(one, jnp.float32) if isinstance(one, tuple) else one for one in scratch],
        compiler_params=pltpu.CompilerParams(vmem_limit_bytes=limit),
        cost_estimate=pl.CostEstimate(flops=200_000_000, bytes_accessed=4_000_000, transcendentals=0),
    )(*tables, *arrays)


def shifted(array, axis, amount):
    count = lax.axis_size(axis)
    return lax.ppermute(array, axis, [(i, (i + amount) % count) for i in range(count)])


def swapped(array, axis, mask):
    count = lax.axis_size(axis)
    return lax.ppermute(array, axis, [(i, i ^ mask) for i in range(count)])


def per_device(
    previous_head,
    recharge,
    soil_zone,
    soil_cond,
    soil_store,
    species,
    mineral_zone,
    rate_table,
    stoich,
    log_equil,
):
    count = lax.axis_size("sp")
    devices = count * lax.axis_size("gx")
    layers, rows, columns = previous_head.shape
    groups = species.shape[0]
    assert columns == LANES and layers == 8 and rows == 8 and count & (count - 1) == 0
    assert 2 * layers * HALO < LANES and 2 * groups * layers <= LANES
    tile = (rows, LANES)
    everywhere = ("gx", "sp")

    field, sides, *blocks = call(
        field_kernel,
        [],
        [soil_cond, soil_store, previous_head, recharge, soil_zone, species],
        [(2 * layers,) + tile, (devices,) + tile] + [(groups * layers + 1,) + tile] * count,
        [pltpu.SMEM(soil_cond.shape, jnp.float32), pltpu.SMEM(soil_store.shape, jnp.float32)]
        + [(layers,) + tile] * 2
        + [pltpu.VMEM((layers,) + tile, jnp.int32), species.shape, pltpu.SemaphoreType.DMA((6,))],
        pltpu.HBM,
        WHOLE_VMEM_BYTES,
    )
    sides = lax.all_to_all(sides, everywhere, 0, 0, tiled=True)
    below = shifted(field, "gx", -1)
    above = shifted(field, "gx", 1)
    arrived = {}
    for d in range(count - 1, 0, -1):
        arrived[d] = swapped(blocks[d], "sp", d)
    blocks = [blocks[0]] + [arrived[d] for d in range(1, count)]
    powers, products = call(powers_kernel, [], [stoich], [(stoich.shape[1],) * 2] * 2)
    extended = (layers, 3 * rows, 2 * LANES)
    basis, kx, ky, kz, scale, sums = call(
        krylov_kernel,
        [soil_cond, soil_store],
        [sides, previous_head, recharge, soil_zone, above, below],
        [(BASIS,) + extended, extended, extended, (layers + 1,) + extended[1:], tile, (devices, LANES)],
        [extended, extended, (PAIR_ROWS, LANES)],
    )
    sums = lax.all_to_all(sums, everywhere, 0, 0, tiled=True)
    rims = call(
        functools.partial(rim_kernel, groups), [], blocks + [scale], [(count * groups, layers, LANES)] * 2
    )
    below, above = shifted(rims[0], "gx", -1), shifted(rims[1], "gx", 1)
    (half_rates,) = call(rates_kernel, [rate_table], [mineral_zone], [(rate_table.shape[1] * layers,) + tile])
    head_field, *reacted = call(
        functools.partial(finish_kernel, groups),
        [stoich, powers, products, log_equil],
        [scale, sums, half_rates, basis, kx, ky, kz, above, below] + blocks,
        [(layers,) + tile] + [(groups * layers,) + tile] * count,
        [extended, (PAIR_ROWS, LANES)],
    )
    arrived = {d: swapped(reacted[d], "sp", d) for d in range(count - 1, 0, -1)}
    (species_out,) = call(place_kernel, [], [reacted[0]] + [arrived[d] for d in range(1, count)], [species.shape])
    return (head_field, species_out)


def solution(mesh):
    in_specs = (
        P(None, "gx", "sp"),
        P(None, "gx", "sp"),
        P(None, "gx", "sp"),
        P(),
        P(),
        P("sp", None, "gx", None),
        P(None, "gx", "sp"),
        P(),
        P(),
        P(),
    )
    out_specs = (P(None, "gx", "sp"), P("sp", None, "gx", None))

    return jax.shard_map(per_device, mesh=mesh, in_specs=in_specs, out_specs=out_specs, check_vma=False)
```

```python
import functools

import jax
import jax.numpy as jnp
from jax import lax
from jax.experimental import pallas as pl
from jax.experimental.pallas import tpu as pltpu
from jax.sharding import PartitionSpec as P


ITERS = 6
NEWTON = 2

time_step = 0.05
dispersion = 0.5
reaction_span = 0.5
newton_damping = 0.5

LANES = 128
VMEM_BYTES = 16 * 1024 * 1024
WHOLE_VMEM_BYTES = 60 * 1024 * 1024
BASIS = ITERS + 1
HALO = ITERS + 1
LAYERS_TOGETHER = 8
PAIRS = [(i, j) for j in range(BASIS) for i in range(j + 1)]
PAIR_AT = {pair: at for at, pair in enumerate(PAIRS)}
PAIR_ROWS = -(-len(PAIRS) // 8) * 8


def harmonic(center, other):
    return 2.0 * center * other / jnp.maximum(center + other, 1e-30)


def pick(labels, table, first):
    value = jnp.zeros(labels.shape, jnp.float32)
    for level in range(table.shape[0]):
        value = jnp.where(labels == level + first, table[level], value)
    return value


def lane_ids(shape):
    return lax.broadcasted_iota(jnp.int32, shape, len(shape) - 1)


def fetch(pairs, sems, later):
    copies = [
        pltpu.make_async_copy(source, target, sems.at[at]) for at, (source, target) in enumerate(pairs + later)
    ]
    for copy in copies:
        copy.start()
    for copy in copies[: len(pairs)]:
        copy.wait()
    return copies[len(pairs) :]


def field_kernel(cond_h, store_h, previous_h, recharge_h, zone_h, species_h, field, sides, *refs):
    *blocks, cond_t, store_t, previous, recharge, zone, species, sems = refs
    (species_copy,) = fetch(
        [(cond_h, cond_t), (store_h, store_t), (previous_h, previous), (recharge_h, recharge), (zone_h, zone)],
        sems,
        [(species_h, species)],
    )
    count = lax.axis_size("sp")
    me = lax.axis_index("sp")
    layers = previous.shape[0]
    shape = previous.shape[1:]
    lane = lane_ids(shape)
    conduct, bound = [], []
    to_left = to_right = jnp.zeros(shape, jnp.float32)
    for z in range(layers):
        labels = zone[z]
        conduct.append(pick(labels, cond_t, 0))
        storage = pick(labels, store_t, 0)
        bound.append(storage)
        values = (storage * previous[z] + recharge[z], (labels + 1).astype(jnp.float32))
        for part, value in enumerate(values):
            at = part * layers + z
            field[at] = value
            here = jnp.logical_and(lane >= at * HALO, lane < (at + 1) * HALO)
            to_left = jnp.where(here, pltpu.roll(value, at * HALO, 1), to_left)
            to_right = jnp.where(here, pltpu.roll(value, (at + 1) * HALO % LANES, 1), to_right)
    power = jnp.zeros(shape, jnp.float32)
    upright = [harmonic(conduct[z], conduct[(z + 1) % layers]) for z in range(layers)]
    for z in range(layers):
        here = conduct[z]
        total = upright[z] + upright[z - 1]
        for axis in range(2):
            face = harmonic(here, pltpu.roll(here, 1, axis))
            total = total + face + pltpu.roll(face, shape[axis] - 1, axis)
        square = bound[z] + 2.0 * total
        square = square * square
        power = power + square * square
    column = jnp.sum(power, axis=0, keepdims=True) * (1.0 / (layers * shape[0]))
    top = jnp.broadcast_to(jnp.max(column, axis=1, keepdims=True), shape)
    for s in range(count):
        tile = jnp.where(me + 1 == s, to_right, jnp.where(me - 1 == s, to_left, 0.0))
        tile = jnp.where(lane >= 2 * layers * HALO, top, tile)
        for g in range(sides.shape[0] // count):
            sides[g * count + s] = tile
    species_copy.wait()
    pack(species, *blocks)


def pack(species, *blocks):
    count = len(blocks)
    me = lax.axis_index("sp")
    groups, layers, rows = species.shape[:3]
    shape = (rows, LANES)
    lane = lane_ids(shape)
    for d in range(count):
        here = jnp.bitwise_xor(me, d)
        sides = (lax.rem(here + count - 1, count), here, lax.rem(here + 1, count))
        at = [pl.ds(pl.multiple_of(i * LANES, LANES), LANES) for i in sides]
        edge = jnp.zeros(shape, jnp.float32)
        for c in range(groups):
            for z in range(layers):
                j = c * layers + z
                blocks[d][j] = species[c, z, :, at[1]]
                ends = jnp.where(lane == 0, species[c, z, :, at[2]], species[c, z, :, at[0]])
                edge = jnp.where(jnp.right_shift(lane, 1) == j, pltpu.roll(ends, 2 * j + 1, 1), edge)
        blocks[d][groups * layers] = edge


def rim_kernel(groups, *refs):
    *blocks, _, up, down = refs
    rows = blocks[0].shape[1]
    layers = (blocks[0].shape[0] - 1) // groups
    for d, block in enumerate(blocks):
        for c in range(groups):
            at = pl.ds(c * layers, layers)
            up[d * groups + c] = block[at, 0, :]
            down[d * groups + c] = block[at, rows - 1, :]


def rates_kernel(rate_t, mineral, half_rates):
    layers = mineral.shape[0]
    for z in range(layers):
        labels = mineral[z]
        masks = [labels == level for level in range(rate_t.shape[0])]
        for m in range(rate_t.shape[1]):
            rate = jnp.zeros(labels.shape, jnp.float32)
            for level, mask in enumerate(masks):
                rate = jnp.where(mask, reaction_span * rate_t[level, m], rate)
            half_rates[m * layers + z] = rate


def powers_kernel(stoich, powers, products):
    values = stoich[...]
    result = lax.dot_general(
        values,
        values,
        (((0,), (0,)), ((), ())),
        precision=lax.Precision.HIGHEST,
        preferred_element_type=jnp.float32,
    )
    powers[...] = result
    products[...] = result[:, :1] * result[:1, :]


def krylov_kernel(cond_t, store_t, sides, previous, recharge, zone, above, below, basis, kx, ky, kz, scale, sums, cond_s, store_s, pair_s):
    tall_count, count = lax.axis_size("gx"), lax.axis_size("sp")
    me, me_s = lax.axis_index("gx"), lax.axis_index("sp")
    layers, tall, wide = cond_s.shape
    rows = tall // 3
    lane = lane_ids((rows, LANES))
    tops = jnp.max(sides[...], axis=0)
    tops = jnp.max(jnp.where(lane >= 2 * layers * HALO, tops, 0.0), axis=0, keepdims=True)
    top = jnp.sqrt(jnp.sqrt(jnp.max(tops, axis=1, keepdims=True)))
    scale[...] = jnp.broadcast_to(4.0 / top, scale.shape)
    twice = jnp.broadcast_to(2.0 / top, (1, wide))
    fourth = jnp.broadcast_to(4.0 / top, (1, wide))

    for part, block in enumerate((above, None, below)):
        there = me + part - 1
        valid = jnp.logical_and(there >= 0, there < tall_count)
        there = jnp.clip(there, 0, tall_count - 1) * count
        keep = valid.astype(jnp.float32)
        keep_left = jnp.logical_and(valid, me_s > 0).astype(jnp.float32)
        keep_right = jnp.logical_and(valid, me_s < count - 1).astype(jnp.float32)
        left = sides[there + jnp.maximum(me_s - 1, 0)] * keep_left
        right = sides[there + jnp.minimum(me_s + 1, count - 1)] * keep_right
        at = slice(part * rows, (part + 1) * rows)
        for z in range(layers):
            near = []
            for j in (z, layers + z):
                value = jnp.where(lane < HALO, pltpu.roll(right, (LANES - j * HALO) % LANES, 1), 0.0)
                value = jnp.where(
                    lane >= LANES - HALO, pltpu.roll(left, LANES - (j + 1) * HALO, 1), value
                )
                near.append(value)
            if block is None:
                field, labels = None, zone[z] + 1
            else:
                field, labels = block[z] * keep, block[layers + z] * keep
            for half, (field, labels) in enumerate(((field, labels), near)):
                cols = slice(half * LANES, (half + 1) * LANES)
                storage = pick(labels, store_t, 1)
                if field is None:
                    field = storage * previous[z] + recharge[z]
                basis[0, z, at, cols] = field
                cond_s[z, at, cols] = pick(labels, cond_t, 1)
                store_s[z, at, cols] = storage
    kz[0] = jnp.zeros((tall, wide), jnp.float32)
    for z in range(layers):
        here = cond_s[z]
        kx[z] = harmonic(here, pltpu.roll(here, tall - 1, 0))
        ky[z] = harmonic(here, pltpu.roll(here, wide - 1, 1))
        if z + 1 < layers:
            kz[z + 1] = harmonic(here, cond_s[z + 1])

    def operate(k):
        flow = None
        for z in range(layers):
            value = basis[k, z]
            along_x = kx[z] * (value - pltpu.roll(value, tall - 1, 0))
            along_y = ky[z] * (value - pltpu.roll(value, wide - 1, 1))
            image = store_s[z] * value
            image = image + (along_x - pltpu.roll(along_x, 1, 0))
            image = image + (along_y - pltpu.roll(along_y, 1, 1))
            if z + 1 < layers:
                along_z = kz[z + 1] * (value - basis[k, z + 1])
                image = image + along_z
            if z:
                image = image - flow
            flow = along_z
            yield z, value, image

    for z, value, image in operate(0):
        basis[1, z] = image * twice - value

    def step(k, carry):
        for z, value, image in operate(k):
            basis[k + 1, z] = image * fourth - 2.0 * value - basis[k - 1, z]
        return carry

    lax.fori_loop(1, ITERS, step, 0)

    totals = [None] * len(PAIRS)
    for z in range(layers):
        values = [basis[k, z, rows : 2 * rows, :LANES] for k in range(BASIS)]
        for at, (i, j) in enumerate(PAIRS):
            term = values[i] * values[j]
            totals[at] = term if z == 0 else totals[at] + term
    pair_s[...] = jnp.zeros(pair_s.shape, jnp.float32)
    for at, total in enumerate(totals):
        pair_s[at : at + 1, :] = jnp.sum(total, axis=0, keepdims=True)
    full = jnp.sum(pair_s[...], axis=1, keepdims=True)
    lane = lane_ids(pair_s.shape)
    row = lax.broadcasted_iota(jnp.int32, pair_s.shape, 0)
    line = jnp.sum(jnp.where(lane == row, full, 0.0), axis=0, keepdims=True)
    sums[...] = jnp.broadcast_to(line, sums.shape)


def galerkin_weights(gram):
    def inner(i, j):
        return gram[PAIR_AT[(min(i, j), max(i, j))]]

    matrix = {}
    for i in range(ITERS):
        for j in range(i + 1):
            if j == 0:
                matrix[(i, j)] = 2.0 * (inner(i, 0) + inner(i, 1))
            else:
                matrix[(i, j)] = inner(i, j + 1) + inner(i, j - 1) + 2.0 * inner(i, j)
    least = [matrix[(i, i)] * 2e-7 for i in range(ITERS)]
    right = [inner(i, 0) for i in range(ITERS)]
    inverse = []
    for j in range(ITERS):
        pivot = matrix[(j, j)]
        good = pivot > least[j]
        inverse.append(jnp.where(good, 1.0 / jnp.where(good, pivot, 1.0), 0.0))
        for i in range(j + 1, ITERS):
            factor = matrix[(i, j)] * inverse[j]
            right[i] = right[i] - factor * right[j]
            for k in range(j + 1, i + 1):
                matrix[(i, k)] = matrix[(i, k)] - factor * matrix[(k, j)]
    for i in reversed(range(ITERS)):
        for k in range(i + 1, ITERS):
            right[i] = right[i] - matrix[(k, i)] * right[k]
        right[i] = right[i] * inverse[i]
    return right


def react(moved, half_rates, powers, products, stoich, rows, log_equil):
    minerals = len(half_rates)
    first = []
    for m in range(minerals):
        total = None
        for value, row in zip(moved, rows):
            term = stoich[row, m] * value
            total = term if total is None else total + term
        first.append(total - log_equil[m])
    shift = None
    for newton_pass in range(NEWTON):
        affinity = first
        if shift is not None:
            affinity = [value - past for value, past in zip(first, image)]
        tangent = [jnp.tanh(value) for value in affinity]
        gap = [rate * value for rate, value in zip(half_rates, tangent)]
        if shift is not None:
            gap = [value - past for value, past in zip(gap, shift)]
        gap = [newton_damping * value for value in gap]
        weight = [rate * (1.0 - value * value) for rate, value in zip(half_rates, tangent)]
        matrix = {(i, j): powers[i, j] for i in range(minerals) for j in range(i + 1)}
        ahead, factors, drawn = [], [], [None] * minerals
        for k in range(minerals):
            scaled = 1.0 / (1.0 + weight[k] * matrix[(k, k)])
            left = gap[k] if k == 0 else gap[k] - weight[k] * drawn[k]
            ahead.append(left * scaled)
            factor = weight[k] * scaled
            factors.append(factor)
            for i in range(k + 1, minerals):
                term = matrix[(i, k)] * ahead[k]
                drawn[i] = term if k == 0 else drawn[i] + term
            for i in range(k + 1, minerals):
                if k == 0:
                    for j in range(1, i + 1):
                        matrix[(i, j)] = powers[i, j] - products[i, j] * factor
                else:
                    part = matrix[(i, k)] * factor
                    for j in range(k + 1, i + 1):
                        matrix[(i, j)] = matrix[(i, j)] - part * matrix[(j, k)]
        step, image = [None] * minerals, [None] * minerals
        for k in reversed(range(minerals)):
            total = None
            for j in range(k + 1, minerals):
                term = matrix[(j, k)] * step[j]
                total = term if total is None else total + term
            step[k] = ahead[k] if total is None else ahead[k] - factors[k] * total
            if newton_pass + 1 < NEWTON:
                parts = [part for part in (drawn[k], total) if part is not None]
                image[k] = sum(parts, matrix[(k, k)] * step[k])
        shift = step if shift is None else [past + value for past, value in zip(shift, step)]
    result = []
    for value, row in zip(moved, rows):
        for m in range(minerals):
            value = value - stoich[row, m] * shift[m]
        result.append(value)
    return result


def finish_kernel(groups, stoich, powers, products, log_equil, scale, sums, half_rates, basis, kx, ky, kz, above, below, *refs):
    count = lax.axis_size("sp")
    blocks, (head_out, *outs, head_s, pair_s) = refs[:count], refs[count:]
    me = lax.axis_index("sp")
    layers, rows = head_out.shape[:2]
    tall, wide = head_s.shape[1:]

    total = jnp.sum(sums[...], axis=0, keepdims=True)
    lane = lane_ids(pair_s.shape)
    row = lax.broadcasted_iota(jnp.int32, pair_s.shape, 0)
    spread = jnp.sum(jnp.where(lane == row, total, 0.0), axis=1, keepdims=True)
    pair_s[...] = jnp.broadcast_to(spread, pair_s.shape)
    gram = [pair_s[at : at + 1, :] for at in range(len(PAIRS))]
    weights = [weight * scale[0:1, :] for weight in galerkin_weights(gram)]
    weights = [jnp.concatenate([weight] * (wide // LANES), axis=1) for weight in weights]
    for z in range(layers):
        value = weights[0] * basis[0, z]
        for k in range(1, ITERS):
            value = value + weights[k] * basis[k, z]
        head_s[z] = value
        head_out[z] = value[rows : 2 * rows, :LANES]

    together = LAYERS_TOGETHER
    shape = (together, rows, LANES)
    lane = lane_ids(shape)
    row = lax.broadcasted_iota(jnp.int32, shape, 1)
    center = slice(rows, 2 * rows)

    def layer(step, carry):
        z = step * together
        here_at = pl.ds(z, together)
        before, after = jnp.maximum(z - 1, 0), jnp.minimum(z + together, layers - 1)

        def beside(ref, base, here):
            first, last = ref[pl.ds(base + before, 1)], ref[pl.ds(base + after, 1)]
            return jnp.concatenate([here[1:], last], axis=0), jnp.concatenate([first, here[:-1]], axis=0)

        value = head_s[here_at, :, :LANES]
        face = kx[here_at, :, :LANES]
        flow = face * (value - pltpu.roll(value, tall - 1, 1))
        faces = [(face[:, center], flow[:, center])]
        faces.append((pltpu.roll(face, 1, 1)[:, center], -pltpu.roll(flow, 1, 1)[:, center]))
        value = head_s[here_at, center, :]
        face = ky[here_at, center, :]
        flow = face * (value - pltpu.roll(value, wide - 1, 2))
        faces.append((face[:, :, :LANES], flow[:, :, :LANES]))
        faces.append((pltpu.roll(face, 1, 2)[:, :, :LANES], -pltpu.roll(flow, 1, 2)[:, :, :LANES]))
        value = value[:, :, :LANES]
        heads = beside(head_s.at[:, center, :LANES], 0, value)
        for shift, other in zip((1, 0), heads):
            face = kz[pl.ds(z + shift, together), center, :LANES]
            faces.append((face, face * (value - other)))
        outward = None
        inward = []
        for face, flow in faces:
            term = jnp.maximum(flow, 0.0) + dispersion * face
            outward = term if outward is None else outward + term
            inward.append(time_step * (dispersion * face - jnp.minimum(flow, 0.0)))
        stay = 1.0 - time_step * outward

        moved, table_rows = [], []
        for d, block in enumerate(blocks):
            group = jnp.bitwise_xor(me, d)
            edge = block[groups * layers]
            for c in range(groups):
                at = c * layers
                here = block[pl.ds(at + z, together)]
                last = [pltpu.roll(edge, LANES - 2 - 2 * (at + z + u), 1) for u in range(together)]
                first = jnp.stack([pltpu.roll(value, 2, 1) for value in last])
                last = jnp.stack(last)
                edge_at = d * groups + c
                lines = [ref[edge_at, here_at, :][:, None, :] for ref in (below, above)]
                following = jnp.where(row == rows - 1, lines[0], pltpu.roll(here, rows - 1, 1))
                preceding = jnp.where(row == 0, lines[1], pltpu.roll(here, 1, 1))
                result = stay * here + inward[0] * following + inward[1] * preceding
                result = result + inward[2] * jnp.where(lane == LANES - 1, last, pltpu.roll(here, LANES - 1, 2))
                result = result + inward[3] * jnp.where(lane == 0, first, pltpu.roll(here, 1, 2))
                over, under = beside(block, at, here)
                moved.append(result + inward[4] * over + inward[5] * under)
                table_rows.append(group * groups + c)
        rates = [half_rates[pl.ds(m * layers + z, together)] for m in range(half_rates.shape[0] // layers)]
        reacted = react(moved, rates, powers, products, stoich, table_rows, log_equil)
        for at, result in enumerate(reacted):
            outs[at // groups][pl.ds((at % groups) * layers + z, together)] = result
        return carry

    lax.fori_loop(0, layers // together, layer, 0)


def place_kernel(*refs):
    *blocks, out = refs
    me = lax.axis_index("sp")
    groups, layers = out.shape[:2]
    for d, block in enumerate(blocks):
        column = pl.multiple_of(jnp.bitwise_xor(me, d) * LANES, LANES)
        for c in range(groups):
            for z in range(layers):
                out[c, z, :, pl.ds(column, LANES)] = block[c * layers + z]


def call(kernel, tables, arrays, out_shapes, scratch=(), space=pltpu.VMEM, limit=VMEM_BYTES):
    smem = pl.BlockSpec(memory_space=pltpu.SMEM)
    vmem = pl.BlockSpec(memory_space=pltpu.VMEM)
    outside = pl.BlockSpec(memory_space=space)
    shapes = [jax.ShapeDtypeStruct(shape, jnp.float32) for shape in out_shapes]
    return pl.pallas_call(
        kernel,
        out_shape=shapes,
        in_specs=[smem] * len(tables) + [outside] * len(arrays),
        out_specs=[vmem] * len(shapes),
        scratch_shapes=[pltpu.VMEM(one, jnp.float32) if isinstance(one, tuple) else one for one in scratch],
        compiler_params=pltpu.CompilerParams(vmem_limit_bytes=limit),
        cost_estimate=pl.CostEstimate(flops=200_000_000, bytes_accessed=4_000_000, transcendentals=0),
    )(*tables, *arrays)


def shifted(array, axis, amount):
    count = lax.axis_size(axis)
    return lax.ppermute(array, axis, [(i, (i + amount) % count) for i in range(count)])


def swapped(array, axis, mask):
    count = lax.axis_size(axis)
    return lax.ppermute(array, axis, [(i, i ^ mask) for i in range(count)])


def per_device(
    previous_head,
    recharge,
    soil_zone,
    soil_cond,
    soil_store,
    species,
    mineral_zone,
    rate_table,
    stoich,
    log_equil,
):
    count = lax.axis_size("sp")
    devices = count * lax.axis_size("gx")
    layers, rows, columns = previous_head.shape
    groups = species.shape[0]
    assert columns == LANES and layers == 8 and rows == 8 and count & (count - 1) == 0
    assert 2 * layers * HALO < LANES and 2 * groups * layers <= LANES
    tile = (rows, LANES)
    everywhere = ("gx", "sp")

    field, sides, *blocks = call(
        field_kernel,
        [],
        [soil_cond, soil_store, previous_head, recharge, soil_zone, species],
        [(2 * layers,) + tile, (devices,) + tile] + [(groups * layers + 1,) + tile] * count,
        [pltpu.SMEM(soil_cond.shape, jnp.float32), pltpu.SMEM(soil_store.shape, jnp.float32)]
        + [(layers,) + tile] * 2
        + [pltpu.VMEM((layers,) + tile, jnp.int32), species.shape, pltpu.SemaphoreType.DMA((6,))],
        pltpu.HBM,
        WHOLE_VMEM_BYTES,
    )
    sides = lax.all_to_all(sides, everywhere, 0, 0, tiled=True)
    below = shifted(field, "gx", -1)
    above = shifted(field, "gx", 1)
    arrived = {}
    for d in range(count - 1, 0, -1):
        arrived[d] = swapped(blocks[d], "sp", d)
    blocks = [blocks[0]] + [arrived[d] for d in range(1, count)]
    powers, products = call(powers_kernel, [], [stoich], [(stoich.shape[1],) * 2] * 2)
    extended = (layers, 3 * rows, 2 * LANES)
    basis, kx, ky, kz, scale, sums = call(
        krylov_kernel,
        [soil_cond, soil_store],
        [sides, previous_head, recharge, soil_zone, above, below],
        [(BASIS,) + extended, extended, extended, (layers + 1,) + extended[1:], tile, (devices, LANES)],
        [extended, extended, (PAIR_ROWS, LANES)],
    )
    sums = lax.all_to_all(sums, everywhere, 0, 0, tiled=True)
    rims = call(
        functools.partial(rim_kernel, groups), [], blocks + [scale], [(count * groups, layers, LANES)] * 2
    )
    below, above = shifted(rims[0], "gx", -1), shifted(rims[1], "gx", 1)
    (half_rates,) = call(rates_kernel, [rate_table], [mineral_zone], [(rate_table.shape[1] * layers,) + tile])
    head_field, *reacted = call(
        functools.partial(finish_kernel, groups),
        [stoich, powers, products, log_equil],
        [scale, sums, half_rates, basis, kx, ky, kz, above, below] + blocks,
        [(layers,) + tile] + [(groups * layers,) + tile] * count,
        [extended, (PAIR_ROWS, LANES)],
    )
    arrived = {}
    for d in range(1, count):
        arrived[d] = swapped(reacted[d], "sp", d)
    (species_out,) = call(place_kernel, [], [reacted[0]] + [arrived[d] for d in range(1, count)], [species.shape])
    return (head_field, species_out)


def solution(mesh):
    in_specs = (
        P(None, "gx", "sp"),
        P(None, "gx", "sp"),
        P(None, "gx", "sp"),
        P(),
        P(),
        P("sp", None, "gx", None),
        P(None, "gx", "sp"),
        P(),
        P(),
        P(),
    )
    out_specs = (P(None, "gx", "sp"), P("sp", None, "gx", None))

    return jax.shard_map(per_device, mesh=mesh, in_specs=in_specs, out_specs=out_specs, check_vma=False)
```
